32 devices in a mesh: leaf: 8 (over y, x, core), rhs: 4 (over z).
Axes of the slice: x: 2, y: 2, z: 4, core: 2. Of those that a mesh axis runs over, the one named last changes fastest.
Arguments:
- coeffs: float32 [2, 64, 32, 128], P(None, 'rhs', 'leaf'), may hold values from -6 to 6
- own_factors: bfloat16 [6, 2, 32, 128, 128], P(None, None, 'leaf'), may hold values from -0.25 to 0.25
- cross_factors: bfloat16 [6, 2, 32, 128, 128], P(None, None, 'leaf'), may hold values from -0.25 to 0.25
- pattern: int32 [6, 32], P(None, 'leaf'), may hold values 0 or 1
- order: int32 [128], replicated, may hold values from 0 to 127, each once
Outputs:
- values: float32 [2, 64, 512, 8], P(None, 'rhs', 'leaf')
The draws below stay inside these ranges and needn't reach their ends.
Inputs may be any that keep to these rules, and one draw needn't show every extreme that they name: order names each of 0 to 127 once.
All inputs are finite; a program needn't handle non-finite values. No bound on the sum of `pattern` on one device may be relied on, other than what follows from the above.
Results may differ from the reference program's by a relative error of at most 0.007.
Values may be sent and summed in bfloat16 or wider, within the bound.
A program may use at most 64 MiB of HBM per device.

```python
import jax
import jax.numpy as jnp
import numpy as np
from jax import lax

R = 128
NRHS = 64
WINDOW_LEVELS = 6
BLK_DEV = 4
NBLK = 32
N_LEAF = 8


def with_ends(array, stream_key, low, high):
    longest = array.shape.index(max(array.shape))
    spots = []
    for shift in (0, 1):
        where = [jax.random.randint(jax.random.fold_in(stream_key, axis), (), 0, length) for axis, length in enumerate(array.shape)]
        where[longest] = (where[longest] + shift) % array.shape[longest]
        spots.append(tuple(where))
    return array.at[spots[0]].set(low).at[spots[1]].set(high)


def steps_of(key, extent, split, low, high):
    def one(axis_at, parts):
        heights = jax.random.uniform(jax.random.fold_in(jax.random.fold_in(key, 6), axis_at), (parts,), jnp.float32, low / len(split), high / len(split))
        return jnp.repeat(jnp.exp(heights), extent[axis_at] // parts).reshape((-1,) + (1,) * (len(extent) - axis_at - 1))

    gain = one(*split[0])
    for cut in split[1:]:
        gain = gain * one(*cut)
    return gain


def gaussian(rng, extent, spread, most, pieces=(), dtype=jnp.bfloat16):
    result = spread * jax.random.normal(rng, extent, jnp.float32)
    if pieces:
        result = result * steps_of(rng, extent, pieces, -0.22, 0.18)
    return jnp.clip(result, -most, most).astype(dtype)


def setup_inputs(seed: int = 0) -> dict:
    seeds = jax.random.split(jax.random.key(seed), 6)
    return {
        "coeffs": gaussian(seeds[0], (2, NRHS, NBLK, R), 1.0, 6.0, ((1, 4), (2, 8)), jnp.float32),
        "own_factors": gaussian(seeds[1], (WINDOW_LEVELS, 2, NBLK, R, R), (4 * R) ** -0.5, 0.25, ((2, 8),)),
        "cross_factors": gaussian(seeds[2], (WINDOW_LEVELS, 2, NBLK, R, R), (4 * R) ** -0.5, 0.25, ((2, 8),)),
        "pattern": with_ends((jax.random.randint(seeds[3], (WINDOW_LEVELS, NBLK), 0, 4) < 3).astype(jnp.int32), jax.random.fold_in(seeds[3], 1), 0, 1),
        "order": jax.random.permutation(seeds[4], R).astype(jnp.int32),
    }


def contract(left_factor, right_factor):
    return jnp.einsum('heq,eqx->hex', left_factor, right_factor, precision=lax.Precision.HIGHEST)


def complex_apply(rounded, factors):
    real_part = contract(rounded[0], factors[0]) - contract(rounded[1], factors[1])
    imag_part = contract(rounded[0], factors[1]) + contract(rounded[1], factors[0])
    return jnp.stack([real_part, imag_part])


def reference(coeffs, own_factors, cross_factors, pattern, order):
    leaf_bits = N_LEAF.bit_length() - 1
    state = coeffs
    for level in range(WINDOW_LEVELS):
        pair_bit = leaf_bits - 1 - level % leaf_bits
        rounded = lax.optimization_barrier(state.astype(jnp.bfloat16)).astype(jnp.float32)
        self_term = complex_apply(rounded, own_factors[level].astype(jnp.float32))
        cross_term = complex_apply(rounded, cross_factors[level].astype(jnp.float32))
        grouped_blocks = cross_term.reshape(2, NRHS, N_LEAF, BLK_DEV, R)
        partner = np.arange(N_LEAF) ^ (1 << pair_bit)
        moved = grouped_blocks[:, :, partner].reshape(cross_term.shape)
        weight_matrix = pattern[level].astype(jnp.float32)[None, None, :, None]
        state = self_term + weight_matrix * moved
    selected_rows = jnp.take(state, order, axis=3)
    grid = selected_rows.reshape(2, NRHS, N_LEAF, BLK_DEV * R)
    return jnp.transpose(grid, (0, 1, 3, 2))
```

```python
import functools

import jax
import jax.numpy as jnp
from jax import lax
from jax.experimental import pallas as pl
from jax.experimental.pallas import tpu as pltpu
from jax.sharding import PartitionSpec as P

MESH = pl.DeviceIdType.MESH


def flip(index, bit):
    step = 1 << bit
    return index + step - 2 * step * ((index // step) % 2)


def stacked(state):
    half = state.shape[0] // 2
    rounded = state.astype(jnp.bfloat16)
    real, imag = rounded[:half], rounded[half:]
    turned = jnp.concatenate([-imag, real], axis=0)
    return jnp.concatenate([rounded, turned], axis=1)


def product(left, right):
    return jnp.dot(left, right, preferred_element_type=jnp.float32)


def window_kernel(
    n, levels, blocks,
    coeffs_hbm, own_hbm, cross_hbm, pattern_ref, order_ref, out_ref,
    coeffs, own, cross, out_box, in_box, folded, mask_out, mask_in, last_out, last_in,
    load_sem, own_sem, cross_sem, send_sem, recv_sem, mask_sem, last_send, last_recv,
):
    me = lax.axis_index("leaf")
    bits = n.bit_length() - 1
    pair_bit = [bits - 1 - level % bits for level in range(levels)]
    last = levels - 1
    rank = own.shape[-1]
    rows = coeffs.shape[0] // blocks
    parts = n // blocks
    chunk = rank // parts

    coeffs_copy = pltpu.make_async_copy(coeffs_hbm, coeffs, load_sem)
    coeffs_copy.start()
    own_copy, cross_copy = [], []
    for level in range(levels):
        cross_copy.append(pltpu.make_async_copy(cross_hbm.at[level], cross.at[level], cross_sem.at[level]))
        own_copy.append(pltpu.make_async_copy(own_hbm.at[level], own.at[level], own_sem.at[level]))
        cross_copy[level].start()
        own_copy[level].start()

    barrier = pltpu.get_barrier_semaphore()
    for delta in range(1, n):
        pl.semaphore_signal(barrier, inc=1, device_id={"leaf": lax.rem(me + delta, n)}, device_id_type=MESH)

    masks = pattern_ref[...].astype(jnp.float32)
    for block in range(blocks):
        mask_out[block : block + 1, :] = jnp.broadcast_to(masks[block : block + 1, last : last + 1], (1, rank))

    def mask_of(level, block):
        return jnp.broadcast_to(masks[block : block + 1, level : level + 1], (1, rank))

    def factor(ref, level, block):
        return ref[level, :, block].reshape(2 * rank, rank)

    def exchange(level, block):
        return pltpu.make_async_remote_copy(
            src_ref=out_box.at[level, block],
            dst_ref=in_box.at[level, block],
            send_sem=send_sem.at[level, block],
            recv_sem=recv_sem.at[level, block],
            device_id={"leaf": flip(me, pair_bit[level])},
            device_id_type=MESH,
        )

    order_row = jnp.broadcast_to(order_ref[...], (8, rank))
    turned_row = pltpu.roll(order_row, chunk, 1)[0:1]
    order_row = order_row[0:1]
    source = lax.broadcasted_iota(jnp.int32, (rank, rank), 0)
    low = lax.broadcasted_iota(jnp.int32, (rank, rank), 1) < chunk
    straight = jnp.where(source == order_row, 1.0, 0.0)
    shifted = jnp.where(source == turned_row, 1.0, 0.0)
    pick_own = jnp.concatenate([jnp.where(low, straight, 0.0), jnp.where(low, shifted, 0.0)], axis=1).astype(jnp.bfloat16)
    pick_cross = jnp.concatenate([jnp.where(low, 0.0, shifted), jnp.where(low, 0.0, straight)], axis=1)

    def fold(block):
        mask = mask_in[block : block + 1, :]
        mask = jnp.concatenate([mask, mask], axis=1)
        pick = jnp.concatenate([pick_own, (pick_cross * mask).astype(jnp.bfloat16)], axis=0)
        both = jnp.concatenate([factor(own, last, block), factor(cross, last, block)], axis=1)
        folded[block] = product(both, pick).astype(jnp.bfloat16)

    mask_copy = pltpu.make_async_remote_copy(
        src_ref=mask_out, dst_ref=mask_in, send_sem=mask_sem.at[0], recv_sem=mask_sem.at[1],
        device_id={"leaf": flip(me, pair_bit[last])}, device_id_type=MESH,
    )

    kept = [None] * blocks
    coeffs_copy.wait()
    for level in range(last):
        cross_copy[level].wait()
        mask = [mask_of(level - 1, block) for block in range(blocks)] if level else None
        for block in range(blocks):
            if level == 0:
                state = coeffs[pl.ds(block, rows, stride=blocks), :]
            else:
                exchange(level - 1, block).wait_recv()
                state = kept[block] + mask[block] * in_box[level - 1, block].astype(jnp.float32)
            left = stacked(state)
            out_box[level, block] = product(left, factor(cross, level, block)).astype(jnp.bfloat16)
            if level == 0 and block == 0:
                pl.semaphore_wait(barrier, n - 1)
                mask_copy.start()
            exchange(level, block).start()
            if block == 0:
                own_copy[level].wait()
            kept[block] = product(left, factor(own, level, block))
        if level == 1:
            mask_copy.wait()
            cross_copy[last].wait()
            own_copy[last].wait()
        if level in (1, 3):
            for block in range(blocks):
                if (block < blocks // 2) == (level == 1):
                    fold(block)

    mask = [mask_of(last - 1, block) for block in range(blocks)]
    for block in range(blocks):
        exchange(last - 1, block).wait_recv()
        state = kept[block] + mask[block] * in_box[last - 1, block].astype(jnp.float32)
        result = product(stacked(state), folded[block]).astype(jnp.bfloat16)
        for part in range(parts):
            target = block * parts + part
            last_out[target] = result[:, part * rank : (part + 1) * rank]

            @pl.when(target != me)
            def _():
                pltpu.make_async_remote_copy(
                    src_ref=last_out.at[target], dst_ref=last_in.at[me],
                    send_sem=last_send.at[target], recv_sem=last_recv.at[me],
                    device_id={"leaf": target}, device_id_type=MESH,
                ).start()

            @pl.when(target == me)
            def _():
                last_in[me] = result[:, part * rank : (part + 1) * rank]

    for level in range(last):
        for block in range(blocks):
            exchange(level, block).wait_send()

    def final(peer):
        return pltpu.make_async_remote_copy(
            src_ref=last_out.at[peer], dst_ref=last_in.at[peer],
            send_sem=last_send.at[peer], recv_sem=last_recv.at[peer],
            device_id={"leaf": peer}, device_id_type=MESH,
        )

    for delta in range(1, n):
        final(lax.rem(me + delta, n)).wait_recv()
    for device in range(n):
        mine = last_in[device].astype(jnp.float32)
        other = last_in[device ^ (1 << pair_bit[last])].astype(jnp.float32)
        value = mine + pltpu.roll(other, rank - chunk, 1)
        out_ref[pl.ds(device, rows, stride=n), :] = value[:, :chunk]
    for delta in range(1, n):
        final(lax.rem(me + delta, n)).wait_send()


def fused(coeffs, own_factors, cross_factors, pattern, order):
    n = lax.axis_size("leaf")
    pair, rhs, blocks, rank = coeffs.shape
    levels = own_factors.shape[0]
    rows = pair * rhs
    chunk = rank * blocks // n
    dma, bf16 = pltpu.SemaphoreType.DMA, jnp.bfloat16
    anywhere, vmem = pl.BlockSpec(memory_space=pl.ANY), pl.BlockSpec(memory_space=pltpu.VMEM)
    out = pl.pallas_call(
        functools.partial(window_kernel, n, levels, blocks),
        out_shape=jax.ShapeDtypeStruct((rows * n, chunk), jnp.float32),
        in_specs=[anywhere, anywhere, anywhere, vmem, vmem],
        out_specs=vmem,
        scratch_shapes=[
            pltpu.VMEM((rows * blocks, rank), jnp.float32),
            pltpu.VMEM(own_factors.shape, bf16),
            pltpu.VMEM(cross_factors.shape, bf16),
            pltpu.VMEM((levels - 1, blocks, rows, rank), bf16),
            pltpu.VMEM((levels - 1, blocks, rows, rank), bf16),
            pltpu.VMEM((blocks, 2 * rank, 2 * rank), bf16),
            pltpu.VMEM((max(blocks, 8), rank), jnp.float32),
            pltpu.VMEM((max(blocks, 8), rank), jnp.float32),
            pltpu.VMEM((n, rows, rank), bf16),
            pltpu.VMEM((n, rows, rank), bf16),
            dma, dma((levels,)), dma((levels,)),
            dma((levels - 1, blocks)), dma((levels - 1, blocks)),
            dma((2,)), dma((n,)), dma((n,)),
        ],
        compiler_params=pltpu.CompilerParams(collective_id=0, has_side_effects=True),
    )(coeffs.reshape(rows * blocks, rank), own_factors, cross_factors, pattern.T, order.reshape(1, rank))
    return jnp.transpose(out.reshape(pair, rhs, n, chunk), (0, 1, 3, 2))


def from_partner(block, axis, bit):
    count = lax.axis_size(axis)
    route = []
    for low in range(count):
        high = low | 1 << bit
        if high != low and high < count:
            route += [(low, high), (high, low)]
    return lax.ppermute(block, axis, route)


def contract(left_factor, right_factor):
    return jnp.einsum("heq,eqx->hex", left_factor, right_factor, preferred_element_type=jnp.float32)


def complex_apply(rounded, factors):
    real_part = contract(rounded[0], factors[0]) - contract(rounded[1], factors[1])
    imag_part = contract(rounded[0], factors[1]) + contract(rounded[1], factors[0])
    return jnp.stack([real_part, imag_part])


def apply_levels(state, own_factors, cross_factors, pattern, leaf_bits):
    for level in range(own_factors.shape[0]):
        pair_bit = leaf_bits - 1 - level % leaf_bits
        rounded = state.astype(jnp.bfloat16)
        self_term = complex_apply(rounded, own_factors[level])
        cross_term = complex_apply(rounded, cross_factors[level])
        incoming = from_partner(cross_term, "leaf", pair_bit)
        weight_matrix = pattern[level].astype(jnp.float32)[None, None, :, None]
        state = self_term + weight_matrix * incoming
    return state


def general(coeffs, own_factors, cross_factors, pattern, order):
    leaf_bits = lax.axis_size("leaf").bit_length() - 1
    local_blocks = coeffs.shape[2]
    state = apply_levels(coeffs, own_factors, cross_factors, pattern, leaf_bits)
    selected_rows = jnp.take(state, order, axis=3)
    flat = selected_rows.reshape(2, selected_rows.shape[1], local_blocks * selected_rows.shape[3], 1)
    return lax.all_to_all(flat, "leaf", split_axis=2, concat_axis=3, tiled=True)


def local(coeffs, own_factors, cross_factors, pattern, order):
    n, blocks = lax.axis_size("leaf"), coeffs.shape[2]
    if n == 2 * blocks and n <= 8 and own_factors.shape[0] == 6:
        return fused(coeffs, own_factors, cross_factors, pattern, order)
    return general(coeffs, own_factors, cross_factors, pattern, order)


def solution(mesh):
    in_specs = (
        P(None, "rhs", "leaf", None),
        P(None, None, "leaf", None, None),
        P(None, None, "leaf", None, None),
        P(None, "leaf"),
        P(),
    )
    out_specs = P(None, "rhs", "leaf", None)
    return jax.shard_map(local, mesh=mesh, in_specs=in_specs, out_specs=out_specs, check_vma=False)
```

```python
import functools

import jax
import jax.numpy as jnp
from jax import lax
from jax.experimental import pallas as pl
from jax.experimental.pallas import tpu as pltpu
from jax.sharding import PartitionSpec as P

MESH = pl.DeviceIdType.MESH
GROUPS = 2


def flip(index, bit):
    step = 1 << bit
    return index + step - 2 * step * ((index // step) % 2)


def stacked(state):
    half = state.shape[0] // 2
    rounded = state.astype(jnp.bfloat16)
    real, imag = rounded[:half], rounded[half:]
    turned = jnp.concatenate([-imag, real], axis=0)
    return jnp.concatenate([rounded, turned], axis=1)


def product(left, right):
    return jnp.dot(left, right, preferred_element_type=jnp.float32)


def window_kernel(
    n, levels, blocks, groups,
    coeffs_hbm, own_hbm, cross_hbm, pattern_hbm, order_hbm, last_in,
    coeffs, own, cross, pattern, order, out_box, in_box, folded, mask_out, mask_in, last_out,
    load_sem, own_sem, cross_sem, send_sem, recv_sem, mask_sem, last_send, last_recv,
):
    me = lax.axis_index("leaf")
    bits = n.bit_length() - 1
    pair_bit = [bits - 1 - level % bits for level in range(levels)]
    last = levels - 1
    rank = own.shape[-1]
    rows = coeffs.shape[0] // blocks
    parts = n // blocks
    chunk = rank // parts
    size = blocks // groups

    barrier = pltpu.get_barrier_semaphore()
    for delta in range(1, n):
        pl.semaphore_signal(barrier, inc=1, device_id={"leaf": lax.rem(me + delta, n)}, device_id_type=MESH)

    coeffs_copy = pltpu.make_async_copy(coeffs_hbm, coeffs, load_sem.at[0])
    pattern_copy = pltpu.make_async_copy(pattern_hbm, pattern, load_sem.at[1])
    order_copy = pltpu.make_async_copy(order_hbm, order, load_sem.at[2])
    own_copy = [pltpu.make_async_copy(own_hbm.at[k], own.at[k], own_sem.at[k]) for k in range(levels)]
    cross_copy = [pltpu.make_async_copy(cross_hbm.at[k], cross.at[k], cross_sem.at[k]) for k in range(levels)]
    coeffs_copy.start()
    cross_copy[0].start()
    pattern_copy.start()
    order_copy.start()
    own_copy[0].start()

    def exchange(level, group):
        span = pl.ds(group * size, size)
        return pltpu.make_async_remote_copy(
            src_ref=out_box.at[level, span],
            dst_ref=in_box.at[level, span],
            send_sem=send_sem.at[level, group],
            recv_sem=recv_sem.at[level, group],
            device_id={"leaf": flip(me, pair_bit[level])},
            device_id_type=MESH,
        )

    def factor(ref, level, block):
        return ref[level, :, block].reshape(2 * rank, rank)

    def mask_of(level, block):
        masks = pattern[...].astype(jnp.float32)
        return jnp.broadcast_to(masks[block : block + 1, level : level + 1], (1, rank))

    def picks():
        order_row = jnp.broadcast_to(order[...], (8, rank))
        turned_row = pltpu.roll(order_row, chunk, 1)[0:1]
        order_row = order_row[0:1]
        source = lax.broadcasted_iota(jnp.int32, (rank, rank), 0)
        low = lax.broadcasted_iota(jnp.int32, (rank, rank), 1) < chunk
        straight = jnp.where(source == order_row, 1.0, 0.0)
        shifted = jnp.where(source == turned_row, 1.0, 0.0)
        pick_own = jnp.concatenate([jnp.where(low, straight, 0.0), jnp.where(low, shifted, 0.0)], axis=1)
        pick_cross = jnp.concatenate([jnp.where(low, 0.0, shifted), jnp.where(low, 0.0, straight)], axis=1)
        return pick_own.astype(jnp.bfloat16), pick_cross

    def fold(block):
        pick_own, pick_cross = picks()
        mask = mask_in[block : block + 1, :]
        mask = jnp.concatenate([mask, mask], axis=1)
        pick = jnp.concatenate([pick_own, (pick_cross * mask).astype(jnp.bfloat16)], axis=0)
        both = jnp.concatenate([factor(own, last, block), factor(cross, last, block)], axis=1)
        folded[block] = product(both, pick).astype(jnp.bfloat16)

    mask_copy = pltpu.make_async_remote_copy(
        src_ref=mask_out, dst_ref=mask_in, send_sem=mask_sem.at[0], recv_sem=mask_sem.at[1],
        device_id={"leaf": flip(me, pair_bit[last])}, device_id_type=MESH,
    )

    kept = [None] * blocks
    left = [None] * blocks

    def states(level, group, mask):
        found = []
        for block in range(group * size, (group + 1) * size):
            if level == 0:
                found.append(coeffs[pl.ds(block, rows, stride=blocks), :])
            else:
                found.append(kept[block] + mask[block] * in_box[level - 1, block].astype(jnp.float32))
        return found

    coeffs_copy.wait()
    cross_copy[0].wait()
    for level in range(last):
        mask = [mask_of(level - 1, block) for block in range(blocks)] if level else None
        for group in range(groups):
            if level:
                exchange(level - 1, group).wait_recv()
            for index, state in enumerate(states(level, group, mask)):
                block = group * size + index
                left[block] = stacked(state)
                out_box[level, block] = product(left[block], factor(cross, level, block)).astype(jnp.bfloat16)
            if level == 0 and group == 0:
                pl.semaphore_wait(barrier, n - 1)
            exchange(level, group).start()
        if level == 0:
            for later in range(1, levels):
                cross_copy[later].start()
                own_copy[later].start()
            pattern_copy.wait()
            order_copy.wait()
            for block in range(blocks):
                mask_out[block : block + 1, :] = mask_of(last, block)
            mask_copy.start()
        own_copy[level].wait()
        for block in range(blocks):
            kept[block] = product(left[block], factor(own, level, block))
        if level == 1:
            mask_copy.wait()
            cross_copy[last].wait()
            own_copy[last].wait()
        if level in (1, 3):
            for block in range(blocks):
                if (block < blocks // 2) == (level == 1):
                    fold(block)
        if level < last - 1:
            cross_copy[level + 1].wait()

    mask = [mask_of(last - 1, block) for block in range(blocks)]
    for group in range(groups):
        exchange(last - 1, group).wait_recv()
        for index, state in enumerate(states(last, group, mask)):
            block = group * size + index
            result = product(stacked(state), folded[block]).astype(jnp.bfloat16)
            for part in range(parts):
                last_out[block * parts + part] = result[:, part * rank : (part + 1) * rank]
        for target in range(group * size * parts, (group + 1) * size * parts):

            @pl.when(target != me)
            def _():
                pltpu.make_async_remote_copy(
                    src_ref=last_out.at[target], dst_ref=last_in.at[me],
                    send_sem=last_send.at[target], recv_sem=last_recv.at[me],
                    device_id={"leaf": target}, device_id_type=MESH,
                ).start()

    last_in[me] = last_out[me]
    for level in range(last):
        for group in range(groups):
            exchange(level, group).wait_send()

    def final(peer):
        return pltpu.make_async_remote_copy(
            src_ref=last_out.at[peer], dst_ref=last_in.at[peer],
            send_sem=last_send.at[peer], recv_sem=last_recv.at[peer],
            device_id={"leaf": peer}, device_id_type=MESH,
        )

    for delta in range(1, n):
        final(lax.rem(me + delta, n)).wait_recv()
    for delta in range(1, n):
        final(lax.rem(me + delta, n)).wait_send()


def assemble_kernel(n, pair_bit, parts_ref, out_ref):
    rank = parts_ref.shape[2]
    rows, chunk = parts_ref.shape[1], out_ref.shape[1]
    for device in range(n):
        mine = parts_ref[device].astype(jnp.float32)
        other = parts_ref[device ^ (1 << pair_bit)].astype(jnp.float32)
        value = mine + pltpu.roll(other, rank - chunk, 1)
        out_ref[pl.ds(device, rows, stride=n), :] = value[:, :chunk]


def fused(coeffs, own_factors, cross_factors, pattern, order):
    n = lax.axis_size("leaf")
    pair, rhs, blocks, rank = coeffs.shape
    levels = own_factors.shape[0]
    rows = pair * rhs
    chunk = rank * blocks // n
    dma, bf16 = pltpu.SemaphoreType.DMA, jnp.bfloat16
    anywhere, vmem = pl.BlockSpec(memory_space=pl.ANY), pl.BlockSpec(memory_space=pltpu.VMEM)
    landed = pl.pallas_call(
        functools.partial(window_kernel, n, levels, blocks, GROUPS),
        out_shape=pltpu.VMEM((n, rows, rank), bf16),
        in_specs=[anywhere] * 5,
        out_specs=vmem,
        scratch_shapes=[
            pltpu.VMEM((rows * blocks, rank), jnp.float32),
            pltpu.VMEM(own_factors.shape, bf16),
            pltpu.VMEM(cross_factors.shape, bf16),
            pltpu.VMEM((blocks, levels), jnp.int32),
            pltpu.VMEM((1, rank), jnp.int32),
            pltpu.VMEM((levels - 1, blocks, rows, rank), bf16),
            pltpu.VMEM((levels - 1, blocks, rows, rank), bf16),
            pltpu.VMEM((blocks, 2 * rank, 2 * rank), bf16),
            pltpu.VMEM((max(blocks, 8), rank), jnp.float32),
            pltpu.VMEM((max(blocks, 8), rank), jnp.float32),
            pltpu.VMEM((n, rows, rank), bf16),
            dma((3,)), dma((levels,)), dma((levels,)),
            dma((levels - 1, GROUPS)), dma((levels - 1, GROUPS)),
            dma((2,)), dma((n,)), dma((n,)),
        ],
        compiler_params=pltpu.CompilerParams(collective_id=0, has_side_effects=True),
    )(coeffs.reshape(rows * blocks, rank), own_factors, cross_factors, pattern.T, order.reshape(1, rank))
    bits = n.bit_length() - 1
    out = pl.pallas_call(
        functools.partial(assemble_kernel, n, bits - 1 - (levels - 1) % bits),
        out_shape=jax.ShapeDtypeStruct((rows * n, chunk), jnp.float32),
        in_specs=[vmem],
        out_specs=vmem,
    )(pltpu.with_memory_space_constraint(landed, pltpu.VMEM))
    return jnp.transpose(out.reshape(pair, rhs, n, chunk), (0, 1, 3, 2))


def from_partner(block, axis, bit):
    count = lax.axis_size(axis)
    route = []
    for low in range(count):
        high = low | 1 << bit
        if high != low and high < count:
            route += [(low, high), (high, low)]
    return lax.ppermute(block, axis, route)


def contract(left_factor, right_factor):
    return jnp.einsum("heq,eqx->hex", left_factor, right_factor, preferred_element_type=jnp.float32)


def complex_apply(rounded, factors):
    real_part = contract(rounded[0], factors[0]) - contract(rounded[1], factors[1])
    imag_part = contract(rounded[0], factors[1]) + contract(rounded[1], factors[0])
    return jnp.stack([real_part, imag_part])


def apply_levels(state, own_factors, cross_factors, pattern, leaf_bits):
    for level in range(own_factors.shape[0]):
        pair_bit = leaf_bits - 1 - level % leaf_bits
        rounded = state.astype(jnp.bfloat16)
        self_term = complex_apply(rounded, own_factors[level])
        cross_term = complex_apply(rounded, cross_factors[level])
        incoming = from_partner(cross_term, "leaf", pair_bit)
        weight_matrix = pattern[level].astype(jnp.float32)[None, None, :, None]
        state = self_term + weight_matrix * incoming
    return state


def general(coeffs, own_factors, cross_factors, pattern, order):
    leaf_bits = lax.axis_size("leaf").bit_length() - 1
    local_blocks = coeffs.shape[2]
    state = apply_levels(coeffs, own_factors, cross_factors, pattern, leaf_bits)
    selected_rows = jnp.take(state, order, axis=3)
    flat = selected_rows.reshape(2, selected_rows.shape[1], local_blocks * selected_rows.shape[3], 1)
    return lax.all_to_all(flat, "leaf", split_axis=2, concat_axis=3, tiled=True)


def local(coeffs, own_factors, cross_factors, pattern, order):
    n, blocks = lax.axis_size("leaf"), coeffs.shape[2]
    if n == 2 * blocks and n <= 8 and own_factors.shape[0] == 6:
        return fused(coeffs, own_factors, cross_factors, pattern, order)
    return general(coeffs, own_factors, cross_factors, pattern, order)


def solution(mesh):
    in_specs = (
        P(None, "rhs", "leaf", None),
        P(None, None, "leaf", None, None),
        P(None, None, "leaf", None, None),
        P(None, "leaf"),
        P(),
    )
    out_specs = P(None, "rhs", "leaf", None)
    return jax.shard_map(local, mesh=mesh, in_specs=in_specs, out_specs=out_specs, check_vma=False)
```
